32 devices in a mesh: particle: 2 (over x), coil: 8 (over z, y), phase: 2 (over core).
Axes of the slice: x: 2, y: 2, z: 4, core: 2. Of those that a mesh axis runs over, the one named last changes fastest.
Arguments:
- position: float32 [256, 16, 4, 384], P('coil', 'phase', 'particle'), parts along dimension 2, may hold values from -6 to 6
- coil_maps: bfloat16 [8, 256, 4, 384], P('coil', None, 'particle'), parts along dimension 2, may hold values from -2 to 2
- kspace_data: bfloat16 [8, 256, 16, 4, 384], P('coil', None, 'phase', 'particle'), parts along dimension 3, may hold values from -1.796875 to 1.796875
- sample_mask: int32 [256, 16], P(None, 'phase'), may hold values 0 or 1
Outputs:
- gradient: float32 [256, 16, 4, 384], P('coil', 'phase', 'particle'), parts along dimension 2
The draws below stay inside these ranges and needn't reach their ends.
There are 2 independent parts, one for each index of `particle`. The reference program is written for one: setup_inputs(seed, part) draws one part's arguments, and reference() takes and returns one part's arrays. A program takes and returns all parts, laid end to end along the dimension named above; an argument that names none is the same for every part. Nothing has to cross between parts.
All inputs are finite; a program needn't handle non-finite values. No bound on the sum of `sample_mask` on one device may be relied on, other than what follows from the above.
Results may differ from the reference program's by a relative error of at most 0.0012.
Values may be sent and summed in bfloat16 or wider, within the bound.
A program may use at most 64 MiB of HBM per device.

```python
import math
import jax
import jax.numpy as jnp
from jax import lax

NA = 256
NB = 192
SLICES = 2
PHASES = 16
COILS = 8


def set_ends(result, key, least, top_value):
    longest = result.shape.index(max(result.shape))
    spots = []
    for shift in (0, 1):
        where = [jax.random.randint(jax.random.fold_in(key, axis), (), 0, length) for axis, length in enumerate(result.shape)]
        where[longest] = (where[longest] + shift) % result.shape[longest]
        spots.append(tuple(where))
    return result.at[spots[0]].set(least).at[spots[1]].set(top_value)


def steps_of(own_key, extent, shards, low, top_value):
    factor_of = 1.0
    for dim, shards_of in shards:
        draws = jax.random.uniform(jax.random.fold_in(jax.random.fold_in(own_key, 6), dim), (shards_of,), jnp.float32, low / len(shards), top_value / len(shards))
        factor_of = factor_of * jnp.repeat(jnp.exp(draws), extent[dim] // shards_of).reshape((-1,) + (1,) * (len(extent) - 1 - dim))
    return factor_of


def scatter_about(stream_key, extent, scale, limit, cuts=(), kind=jnp.bfloat16):
    loudness = steps_of(stream_key, extent, cuts, -0.22, 0.18) if cuts else 1.0
    drawn = jax.random.normal(stream_key, extent, jnp.float32) * scale * loudness
    return jnp.minimum(jnp.maximum(drawn, -limit), limit).astype(kind)


def setup_inputs(seed: int = 0, part: int = 0) -> dict:
    streams_of = jax.random.split(jax.random.key(seed), 5)
    own_keys = jax.random.split(jax.random.fold_in(streams_of[4], part), 5)
    position = scatter_about(own_keys[0], (NA, PHASES, SLICES, 2 * NB), 1.0, 6.0, ((0, 8), (1, 2)), jnp.float32)
    coil_maps = scatter_about(own_keys[1], (COILS, NA, SLICES, 2 * NB), COILS ** -0.5, 2.0, ((0, 8),))
    kspace_data = scatter_about(own_keys[2], (COILS, NA, PHASES, SLICES, 2 * NB), 0.3, 1.796875, ((0, 8), (2, 2)))
    sample_mask = set_ends((jax.random.randint(streams_of[3], (NA, PHASES), 0, 3) < 1).astype(jnp.int32), jax.random.fold_in(streams_of[3], 1), 0, 1)
    return dict(position=position, coil_maps=coil_maps, kspace_data=kspace_data, sample_mask=sample_mask)


def dft_tables(length):
    counter = jnp.arange(length, dtype=jnp.int32)
    product = counter[:, None] * counter[None, :] % length
    angles = product.astype(jnp.float32) * (2.0 * math.pi / length)
    scaling = 1.0 / math.sqrt(length)
    return (jnp.cos(angles) * scaling, -jnp.sin(angles) * scaling)

def build_tables(rows_total, width):
    row_real, row_imag = dft_tables(rows_total)
    col_real, col_imag = dft_tables(width)
    forward_wide = jnp.concatenate([jnp.concatenate([col_real, col_imag], 1), jnp.concatenate([-col_imag, col_real], 1)], 0)
    backward_wide = jnp.concatenate([jnp.concatenate([col_real, -col_imag], 1), jnp.concatenate([col_imag, col_real], 1)], 0)
    return (row_real.astype(jnp.bfloat16), row_imag.astype(jnp.bfloat16), forward_wide.astype(jnp.bfloat16), backward_wide.astype(jnp.bfloat16))

def complex_times(factor, values, conjugate):
    width = values.shape[-1] // 2
    factor_real = factor[..., :width]
    factor_imag = factor[..., width:]
    if conjugate:
        factor_imag = -factor_imag
    value_real = values[..., :width]
    value_imag = values[..., width:]
    out_real = factor_real * value_real - factor_imag * value_imag
    out_imag = factor_real * value_imag + factor_imag * value_real
    return jnp.concatenate([out_real, out_imag], -1)

def rows_apply(table_real, table_imag, values, adjoint):
    width = values.shape[-1] // 2
    real_part = jnp.einsum('kn,npsd->kpsd', table_real.astype(jnp.float32), values.astype(jnp.float32))
    imag_part = jnp.einsum('kn,npsd->kpsd', table_imag.astype(jnp.float32), values.astype(jnp.float32))
    if adjoint:
        out_real = real_part[..., :width] + imag_part[..., width:]
        out_imag = real_part[..., width:] - imag_part[..., :width]
    else:
        out_real = real_part[..., :width] - imag_part[..., width:]
        out_imag = real_part[..., width:] + imag_part[..., :width]
    return jnp.concatenate([out_real, out_imag], -1)

def reference(position, coil_maps, kspace_data, sample_mask):
    rows_total = position.shape[0]
    width = position.shape[3] // 2
    row_real, row_imag, forward_wide, backward_wide = build_tables(rows_total, width)
    position_low = position.astype(jnp.bfloat16)
    sample_weight = sample_mask.astype(jnp.float32)[:, :, None, None]

    def per_coil(total, inputs):
        coil_map, coil_data = inputs
        map_wide = coil_map.astype(jnp.float32)[:, None]
        lifted = complex_times(map_wide, position_low.astype(jnp.float32), False).astype(jnp.bfloat16)
        spread = jnp.einsum('npsc,cd->npsd', lifted.astype(jnp.float32), forward_wide.astype(jnp.float32)).astype(jnp.bfloat16)
        kspace = rows_apply(row_real, row_imag, spread, False)
        residual = (sample_weight * (kspace - coil_data.astype(jnp.float32))).astype(jnp.bfloat16)
        back_rows = rows_apply(row_real, row_imag, residual, True).astype(jnp.bfloat16)
        back = jnp.einsum('npsc,cd->npsd', back_rows.astype(jnp.float32), backward_wide.astype(jnp.float32))
        return (total + complex_times(map_wide, back, True), None)
    zeros = jnp.zeros(position.shape, jnp.float32)
    likelihood, unused = lax.scan(per_coil, zeros, (coil_maps, kspace_data))
    phase_part = 2.0 * position - jnp.roll(position, 1, axis=1) - jnp.roll(position, -1, axis=1)
    row_part = 2.0 * position - jnp.roll(position, 1, axis=0) - jnp.roll(position, -1, axis=0)
    return 0.6 * likelihood + 0.5 * phase_part + 0.3 * row_part
```

```python
import math

import jax
import jax.numpy as jnp
from jax import lax
from jax.sharding import PartitionSpec as P


def with_halo(block, sides, width):
    for axis, dim in sides:
        count = lax.axis_size(axis)
        forward = [(i, i + 1) for i in range(count - 1)]
        forward.append((count - 1, 0))
        backward = [(target, source) for source, target in forward]
        low = lax.ppermute(
            lax.slice_in_dim(block, block.shape[dim] - width, None, axis=dim), axis, forward
        )
        high = lax.ppermute(lax.slice_in_dim(block, 0, width, axis=dim), axis, backward)
        block = jnp.concatenate([low, block, high], axis=dim)
    return block


def dft_tables(length):
    counter = jnp.arange(length, dtype=jnp.int32)
    product = counter[:, None] * counter[None, :] % length
    angles = product.astype(jnp.float32) * (2.0 * math.pi / length)
    scaling = 1.0 / math.sqrt(length)
    return (jnp.cos(angles) * scaling, -jnp.sin(angles) * scaling)


def build_tables(rows_total, width):
    row_real, row_imag = dft_tables(rows_total)
    col_real, col_imag = dft_tables(width)
    forward_wide = jnp.concatenate(
        [jnp.concatenate([col_real, col_imag], 1), jnp.concatenate([-col_imag, col_real], 1)], 0
    )
    backward_wide = jnp.concatenate(
        [jnp.concatenate([col_real, -col_imag], 1), jnp.concatenate([col_imag, col_real], 1)], 0
    )
    return (
        row_real.astype(jnp.bfloat16),
        row_imag.astype(jnp.bfloat16),
        forward_wide.astype(jnp.bfloat16),
        backward_wide.astype(jnp.bfloat16),
    )


def complex_times(factor, values, conjugate):
    width = values.shape[-1] // 2
    factor_real = factor[..., :width]
    factor_imag = factor[..., width:]
    if conjugate:
        factor_imag = -factor_imag
    value_real = values[..., :width]
    value_imag = values[..., width:]
    out_real = factor_real * value_real - factor_imag * value_imag
    out_imag = factor_real * value_imag + factor_imag * value_real
    return jnp.concatenate([out_real, out_imag], -1)


def rows_apply(table_real, table_imag, values, adjoint):
    width = values.shape[-1] // 2
    real_part = jnp.einsum("kn,npsd->kpsd", table_real, values, preferred_element_type=jnp.float32)
    imag_part = jnp.einsum("kn,npsd->kpsd", table_imag, values, preferred_element_type=jnp.float32)
    if adjoint:
        out_real = real_part[..., :width] + imag_part[..., width:]
        out_imag = real_part[..., width:] - imag_part[..., :width]
    else:
        out_real = real_part[..., :width] - imag_part[..., width:]
        out_imag = real_part[..., width:] + imag_part[..., :width]
    return jnp.concatenate([out_real, out_imag], -1)


def local(position, coil_maps, kspace_data, sample_mask):
    rows_total = coil_maps.shape[1]
    width = position.shape[3] // 2
    row_real, row_imag, forward_wide, backward_wide = build_tables(rows_total, width)
    coil_map = coil_maps[0]
    coil_data = kspace_data[0]
    sample_weight = sample_mask.astype(jnp.float32)[:, :, None, None]
    position_low = position.astype(jnp.bfloat16)
    map_rows = coil_map.astype(jnp.float32)[:, None]
    lifted = complex_times(
        map_rows,
        lax.all_gather(position_low, "coil", axis=0, tiled=True).astype(jnp.float32),
        False,
    ).astype(jnp.bfloat16)
    spread = jnp.einsum(
        "npsc,cd->npsd", lifted, forward_wide, preferred_element_type=jnp.float32
    ).astype(jnp.bfloat16)
    kspace = rows_apply(row_real, row_imag, spread, False)
    residual = (sample_weight * (kspace - coil_data.astype(jnp.float32))).astype(jnp.bfloat16)
    back_rows = rows_apply(row_real, row_imag, residual, True).astype(jnp.bfloat16)
    back = jnp.einsum("npsc,cd->npsd", back_rows, backward_wide, preferred_element_type=jnp.float32)
    map_rows = coil_map.astype(jnp.float32)[:, None]
    partial = complex_times(map_rows, back, True).astype(jnp.bfloat16)
    likelihood = lax.psum_scatter(partial, "coil", scatter_dimension=0, tiled=True).astype(jnp.float32)
    padded = with_halo(position, (("coil", 0), ("phase", 1)), 1)
    phase_part = 2.0 * position - padded[1:-1, :-2] - padded[1:-1, 2:]
    row_part = 2.0 * position - padded[:-2, 1:-1] - padded[2:, 1:-1]
    return 0.6 * likelihood + 0.5 * phase_part + 0.3 * row_part


def solution(mesh):
    in_specs = (
        P("coil", "phase", "particle", None),
        P("coil", None, "particle", None),
        P("coil", None, "phase", "particle", None),
        P(None, "phase"),
    )
    out_specs = P("coil", "phase", "particle", None)
    return jax.shard_map(local, mesh=mesh, in_specs=in_specs, out_specs=out_specs, check_vma=False)
```
